32 devices in a mesh: groups: 2 (over y), ctx: 4 (over z), state: 2 (over x), head: 2 (over core).
Axes of the slice: x: 2, y: 2, z: 4, core: 2. Of those that a mesh axis runs over, the one named last changes fastest.
Arguments:
- x_in: bfloat16 [4096, 4096], P(('groups', 'ctx'), 'head'), parts along dimension 0, may hold values from -6 to 6
- b_in: bfloat16 [4096, 1024], P(('groups', 'ctx'), 'state'), parts along dimension 0, may hold values from -6 to 6
- c_in: bfloat16 [4096, 1024], P(('groups', 'ctx'), 'state'), parts along dimension 0, may hold values from -6 to 6
- z_in: bfloat16 [4096, 4096], P(('groups', 'ctx'), ('head', 'state')), parts along dimension 0, may hold values from -6 to 6
- dt_raw: float32 [4096, 64], P(('groups', 'ctx'), 'head'), parts along dimension 0, may hold values from -5 to 5
- decay_rate: float32 [64], P('head'), may hold values from 0.00012207031 to 0.05, as said below
- d_skip: float32 [64], P('head'), may hold values from 0.5 to 1.5
- conv_x: float32 [4, 4096], P(None, 'head'), may hold values from -3 to 3
- conv_b: float32 [4, 1024], P(None, 'state'), may hold values from -0.3 to 0.3
- conv_c: float32 [4, 1024], P(None, 'state'), may hold values from -0.3 to 0.3
- norm_gain: float32 [4096], P(('head', 'state')), may hold values from 0.5 to 1.5
- w_out: bfloat16 [4096, 4096], P('ctx', ('state', 'head')), may hold values from -0.09375 to 0.09375
Outputs:
- layer_out: bfloat16 [4096, 4096], P(('groups', 'ctx'), ('state', 'head')), parts along dimension 0
The draws below stay inside these ranges and needn't reach their ends.
There are 2 independent parts, one for each index of `groups`. The reference program is written for one: setup_inputs(seed, part) draws one part's arguments, and reference() takes and returns one part's arrays. A program takes and returns all parts, laid end to end along the dimension named above; an argument that names none is the same for every part. Nothing has to cross between parts.
Inputs may be any that keep to these rules, and one draw needn't show every extreme that they name: `decay_rate`: positive decay rate of each head.
All inputs are finite; a program needn't handle non-finite values.
Results may differ from the reference program's by a relative error of at most 0.014.
Values may be sent and summed in bfloat16 or wider, within the bound.
No kernel may reach another device: no remote copies, remote signals or barrier semaphores. Data moves between devices by JAX's collectives and lax.ppermute only.
A program may use at most 128 MiB of HBM per device.

```python
import math
import jax
import jax.numpy as jnp
from jax import lax

D = 4096
HEADS = 64
P_SIZE = 64
NSTATE = 1024
SPAN = 256
KW = 4
TOK_DEV = 512
CH = 4096
TOKENS = 2048


def draw_decay_rate(key, part):
    lowest = math.log(0.25 / TOKENS)
    highest = math.log(0.05)
    key_one = jax.random.fold_in(key, 0)
    return jnp.exp(jax.random.uniform(key_one, (HEADS,), jnp.float32, lowest, highest)).astype(jnp.float32)


def draw_dt_raw(key, part):
    key_one, key_two = jax.random.split(jax.random.fold_in(key, 17))
    block_count = TOKENS // TOK_DEV
    offsets = jax.random.uniform(key_one, (block_count, 1, HEADS), jnp.float32, -2.0, 2.0)
    rough = jnp.clip(0.7 * jax.random.normal(key_two, (block_count, TOK_DEV, HEADS), jnp.float32), -3.0, 3.0)
    return (offsets + rough).reshape(TOKENS, HEADS).astype(jnp.float32)


def block_levels(rng, dims, cuts, least, largest):
    gain, own = 1.0, jax.random.fold_in(rng, 6)
    for dim, blocks in cuts:
        steps = jnp.exp(jax.random.uniform(jax.random.fold_in(own, dim), (blocks,), jnp.float32, least / len(cuts), largest / len(cuts)))
        gain = gain * jnp.repeat(steps, dims[dim] // blocks).reshape([-1 if axis == dim else 1 for axis in range(len(dims))])
    return gain


def gaussian(key, dims, deviation, most, cuts=(), dtype=jnp.bfloat16):
    array = jax.random.normal(key, dims, jnp.float32) * deviation
    if len(cuts) > 0:
        array = block_levels(key, dims, cuts, -0.22, 0.18) * array
    return jnp.clip(array, min=-most, max=most).astype(dtype)


def setup_inputs(seed: int = 0, part: int = 0) -> dict:
    streams_of = jax.random.split(jax.random.key(seed), 13)
    part_keys = jax.random.split(jax.random.fold_in(streams_of[12], part), 13)
    x_in = gaussian(part_keys[0], (TOKENS, CH), 1.0, 6.0, ((0, 4), (1, 2)))
    b_in = gaussian(part_keys[1], (TOKENS, NSTATE), 1.0, 6.0, ((0, 4), (1, 2)))
    c_in = gaussian(part_keys[2], (TOKENS, NSTATE), 1.0, 6.0, ((0, 4), (1, 2)))
    z_in = gaussian(part_keys[3], (TOKENS, CH), 1.0, 6.0, ((0, 4), (1, 4)))
    dt_raw = draw_dt_raw(jax.random.fold_in(jax.random.fold_in(streams_of[12], part), 71), part)
    decay_rate = draw_decay_rate(jax.random.fold_in(streams_of[12], 71), part)
    d_skip = jnp.clip(0.5 + 1.0 * jax.random.uniform(streams_of[6], (HEADS,), jnp.float32) ** block_levels(streams_of[6], (HEADS,), ((0, 2),), -0.2, 0.2), 0.5, 1.5)
    conv_x = gaussian(streams_of[7], (KW, CH), 0.5, 3.0, ((1, 2),), jnp.float32)
    conv_b = gaussian(streams_of[8], (KW, NSTATE), 0.05, 0.3, ((1, 2),), jnp.float32)
    conv_c = gaussian(streams_of[9], (KW, NSTATE), 0.05, 0.3, ((1, 2),), jnp.float32)
    norm_gain = jnp.clip(0.5 + 1.0 * jax.random.uniform(streams_of[10], (CH,), jnp.float32) ** block_levels(streams_of[10], (CH,), ((0, 4),), -0.2, 0.2), 0.5, 1.5)
    w_out = gaussian(streams_of[11], (CH, D), CH ** -0.5, 0.09375, ((0, 4), (1, 4)))
    return dict(x_in=x_in, b_in=b_in, c_in=c_in, z_in=z_in, dt_raw=dt_raw, decay_rate=decay_rate, d_skip=d_skip, conv_x=conv_x, conv_b=conv_b, conv_c=conv_c, norm_gain=norm_gain, w_out=w_out)


def conv_silu(signal, before, weights):
    length = signal.shape[0]
    tap_count = weights.shape[0]
    joined = jnp.concatenate([before, signal], axis=0).astype(jnp.float32)
    summed = weights[tap_count - 1] * joined[tap_count - 1:]
    for tap_index in range(tap_count - 1):
        summed = summed + weights[tap_index] * joined[tap_index:tap_index + length]
    return jax.nn.silu(summed).astype(jnp.bfloat16)

def reference(x_in, b_in, c_in, z_in, dt_raw, decay_rate, d_skip, conv_x, conv_b, conv_c, norm_gain, w_out):
    tap_count = conv_x.shape[0]
    x_conv = conv_silu(x_in, jnp.zeros((tap_count - 1, CH), jnp.bfloat16), conv_x)
    b_conv = conv_silu(b_in, jnp.zeros((tap_count - 1, NSTATE), jnp.bfloat16), conv_b)
    c_conv = conv_silu(c_in, jnp.zeros((tap_count - 1, NSTATE), jnp.bfloat16), conv_c)
    span_count = TOKENS // SPAN
    step_size = jax.nn.softplus(dt_raw).reshape(span_count, SPAN, HEADS)
    x_blocks = x_conv.reshape(span_count, SPAN, HEADS, P_SIZE)
    b_blocks = b_conv.reshape(span_count, SPAN, NSTATE)
    c_blocks = c_conv.reshape(span_count, SPAN, NSTATE)
    causal = jnp.arange(SPAN)[:, None] >= jnp.arange(SPAN)[None, :]
    highest = lax.Precision.HIGHEST

    def one_span(state_now, pieces):
        x_piece, b_piece, c_piece, step_piece = pieces
        cumulative = jnp.cumsum(-decay_rate * step_piece, axis=0)
        span_total = cumulative[-1]
        x_float = x_piece.astype(jnp.float32)
        inner_all = jnp.dot(c_piece, b_piece.T, preferred_element_type=jnp.float32)
        cum_heads = cumulative.T
        log_gap = cum_heads[:, :, None] - cum_heads[:, None, :]
        scores = (inner_all[None] * jnp.exp(jnp.where(causal, log_gap, -jnp.inf))).astype(jnp.bfloat16)
        scores = lax.optimization_barrier(scores)
        inputs = (step_piece[:, :, None] * x_float).astype(jnp.bfloat16)
        inputs = lax.optimization_barrier(inputs)
        intra = jnp.einsum('hts,shp->thp', scores.astype(jnp.float32), inputs.astype(jnp.float32), precision=highest)
        states_b = lax.optimization_barrier(state_now.astype(jnp.bfloat16))
        inter = jnp.einsum('tn,hpn->thp', c_piece.astype(jnp.float32), states_b.astype(jnp.float32), precision=highest)
        inter = inter * jnp.exp(cumulative)[:, :, None]
        weighted = ((jnp.exp(span_total[None] - cumulative) * step_piece)[:, :, None] * x_float).astype(jnp.bfloat16)
        weighted = lax.optimization_barrier(weighted)
        update = jnp.einsum('thp,tn->hpn', weighted.astype(jnp.float32), b_piece.astype(jnp.float32), precision=highest)
        state_next = jnp.exp(span_total)[:, None, None] * state_now + update
        result = intra + d_skip[None, :, None] * x_float + inter
        return (state_next, result)
    start_state = jnp.zeros((HEADS, P_SIZE, NSTATE), jnp.float32)
    final_state, outputs = lax.scan(one_span, start_state, (x_blocks, b_blocks, c_blocks, step_size))
    mixed = outputs.reshape(TOKENS, CH)
    gated = mixed * jax.nn.silu(z_in.astype(jnp.float32))
    mean_square = lax.optimization_barrier(jnp.sum(gated * gated, axis=1)) / CH
    normed = (gated * lax.rsqrt(mean_square + 1e-05)[:, None] * norm_gain).astype(jnp.bfloat16)
    return jnp.dot(normed, w_out, preferred_element_type=jnp.float32).astype(jnp.bfloat16)
```

```python
import functools

import jax
import jax.numpy as jnp
from jax import lax
from jax.experimental import pallas as pl
from jax.experimental.pallas import tpu as pltpu
from jax.sharding import PartitionSpec as P

BF = jnp.bfloat16
F32 = jnp.float32
LANES = 128
HALO = 16
VM = pl.BlockSpec(memory_space=pltpu.VMEM)
SM = pl.BlockSpec(memory_space=pltpu.SMEM)
ANY = pl.BlockSpec(memory_space=pl.ANY)
PARAMS = pltpu.CompilerParams(vmem_limit_bytes=56 * 1024 * 1024)


def line(n, d):
    return [(i, i + d) for i in range(n) if 0 <= i + d < n]


def ring(n, d):
    return [(i, (i + d) % n) for i in range(n)]


def expand(v, head_size):
    per = LANES // head_size
    lane = lax.broadcasted_iota(jnp.int32, (v.shape[0], LANES), 1)
    cols = []
    for p in range(v.shape[1] // per):
        e = jnp.broadcast_to(v[:, p * per : p * per + 1], lane.shape)
        for q in range(1, per):
            e = jnp.where(lane < q * head_size, e, v[:, p * per + q : p * per + q + 1])
        cols.append(e)
    return cols[0] if len(cols) == 1 else jnp.concatenate(cols, axis=1)


def silu(v):
    return v / (1.0 + jnp.exp(-v))


def dot(a, b):
    return jnp.dot(a, b, preferred_element_type=F32)


def steps_kernel(dt_ref, decay_ref, step_ref, cum_ref, cumt_ref):
    dt = dt_ref[...]
    step = jnp.maximum(dt, 0.0) + jnp.log1p(jnp.exp(-jnp.abs(dt)))
    cum = -decay_ref[...] * step
    row = lax.broadcasted_iota(jnp.int32, cum.shape, 0)
    d = 1
    while d < cum.shape[0]:
        cum = cum + jnp.where(row >= d, pltpu.roll(cum, d, 0), 0.0)
        d *= 2
    step_ref[...] = step
    cum_ref[...] = cum
    cumt_ref[...] = cum.T


def conv_block(signal, halo, taps):
    k = taps.shape[0]
    xf = signal.astype(F32)
    hf = halo.astype(F32)
    row = lax.broadcasted_iota(jnp.int32, (8, xf.shape[1]), 0)
    total = taps[k - 1 : k, :] * xf
    for d in range(1, k):
        r = pltpu.roll(xf, d, 0)
        h = pltpu.roll(hf, d, 0)
        top = jnp.where(row < d, h[:8], r[:8])
        total = total + taps[k - 1 - d : k - d, :] * jnp.concatenate([top, r[8:]], axis=0)
    return silu(total).astype(BF)


def conv_kernel(sc, x_ref, b_ref, c_ref, halo_ref, tx_ref, tb_ref, tc_ref, xo_ref, bc_ref, part_ref):
    width = x_ref.shape[1]
    nb = b_ref.shape[1]
    w = min(256, nb)
    for j in range(0, nb, w):
        s = slice(j, j + w)
        bc_ref[:, s] = conv_block(b_ref[:, s], halo_ref[:, width + j : width + j + w], tb_ref[:, s])
        bc_ref[:, nb + j : nb + j + w] = conv_block(
            c_ref[:, s], halo_ref[:, width + nb + j : width + nb + j + w], tc_ref[:, s]
        )
    rows = part_ref.shape[0]
    part_ref[...] = bc_ref[pl.ds(pl.multiple_of(sc[1] * rows, rows), rows), :]
    for j in range(0, width, w):
        s = slice(j, j + w)
        xo_ref[:, s] = conv_block(x_ref[:, s], halo_ref[:, s], tx_ref[:, s])


def states_kernel(n_pieces, n_chunks, head_size, x_ref, step_ref, cum_ref, *refs):
    bcs = refs[:n_pieces]
    dec_ref = refs[n_pieces]
    full = refs[n_pieces + 1 : n_pieces + 1 + n_chunks]
    half = refs[n_pieces + 1 + n_chunks :]
    tok = x_ref.shape[0]
    cum = cum_ref[...]
    last = cum[tok - 1 : tok, :]
    dec_ref[...] = expand(jnp.exp(last), head_size)
    weight = jnp.exp(last - cum) * step_ref[...]
    hc = weight.shape[1] // n_chunks
    w = hc * head_size
    nb = bcs[0].shape[1] // 2
    for c in range(n_chunks):
        weighted = (
            expand(weight[:, c * hc : (c + 1) * hc], head_size)
            * x_ref[:, c * w : (c + 1) * w].astype(F32)
        ).astype(BF)
        for j in range(n_pieces):
            out = lax.dot_general(
                bcs[j][:, :nb], weighted, (((0,), (0,)), ((), ())), preferred_element_type=F32
            )
            full[c][j * nb : (j + 1) * nb, :] = out
            half[c][j * nb : (j + 1) * nb, :] = out.astype(BF)


def intra_kernel(n_pieces, head_size, x_ref, step_ref, cum_ref, cumt_ref, skip_ref, *refs):
    bcs = refs[:n_pieces]
    out_ref, g_ref, in_ref = refs[n_pieces:]
    tok, width = x_ref.shape
    heads = step_ref.shape[1]
    nb = bcs[0].shape[1] // 2
    q = 128
    g = None
    for j in range(n_pieces):
        part = lax.dot_general(
            bcs[j][:, nb:], bcs[j][:, :nb], (((1,), (1,)), ((), ())), preferred_element_type=F32
        )
        g = part if g is None else g + part
    g_ref[...] = g
    xf = x_ref[...].astype(F32)
    out_ref[...] = expand(skip_ref[...], head_size) * xf
    in_ref[...] = (expand(step_ref[...], head_size) * xf).astype(BF)
    causal = lax.broadcasted_iota(jnp.int32, (q, q), 0) >= lax.broadcasted_iota(jnp.int32, (q, q), 1)
    per = LANES // head_size
    for i in range(tok // q):
        r = slice(i * q, (i + 1) * q)
        gd = g_ref[r, r]
        for p in range(heads // per):
            outs = []
            for h in range(p * per, (p + 1) * per):
                gap = cum_ref[r, h : h + 1] - cumt_ref[h : h + 1, r]
                score = (gd * jnp.exp(jnp.where(causal, gap, -jnp.inf))).astype(BF)
                outs.append(dot(score, in_ref[r, h * head_size : (h + 1) * head_size]))
            s = slice(p * LANES, (p + 1) * LANES)
            out_ref[r, s] += jnp.concatenate(outs, axis=1)
    size = q
    while size < tok:
        for lo in range(0, tok, 2 * size):
            a = slice(lo, lo + size)
            b = slice(lo + size, lo + 2 * size)
            pivot = cum_ref[lo + size - 1 : lo + size, :]
            right = (
                expand(jnp.exp(pivot - cum_ref[a, :]) * step_ref[a, :], head_size)
                * x_ref[a, :].astype(F32)
            ).astype(BF)
            out_ref[b, :] += expand(jnp.exp(cum_ref[b, :] - pivot), head_size) * dot(
                g_ref[b, a].astype(BF), right
            )
        size *= 2


def last_hop_kernel(has_r, n, *refs):
    c_ref, l_ref, dec_ref = refs[:3]
    e = l_ref[...]
    if has_r:
        e = e + dec_ref[...] * refs[3][...].astype(F32)
    refs[-1][...] = dot(c_ref[...], e.astype(BF)).astype(BF)


def gate_kernel(n_pieces, n_enter, n_chunks, head_size, first, final, *refs):
    refs = list(refs)
    bcs = [refs.pop(0) for _ in range(n_pieces)]
    cum_ref, base_ref, z_ref, gain_ref = [refs.pop(0) for _ in range(4)]
    enters = [[refs.pop(0) for _ in range(n_enter)] for _ in range(n_chunks)]
    lasts = [refs.pop(0) for _ in range(n_chunks)]
    prev = refs.pop(0) if not first else None
    out_ref = refs.pop(0)
    ss_ref = refs.pop(0) if not final else None
    nb = bcs[0].shape[1] // 2
    w = lasts[0].shape[1]
    hc = w // head_size
    total = None
    for c in range(n_chunks):
        s = slice(c * w, (c + 1) * w)
        y = lasts[c][...].astype(F32)
        if n_enter:
            e = enters[c][0][...]
            for other in enters[c][1:]:
                e = e + other[...]
            for j in range(n_pieces):
                y = y + dot(bcs[j][:, nb:], e[j * nb : (j + 1) * nb])
        decay = jnp.exp(cum_ref[:, c * hc : (c + 1) * hc])
        gated = (base_ref[:, s] + expand(decay, head_size) * y) * silu(z_ref[:, s].astype(F32))
        out_ref[:, s] = (gated * gain_ref[:, s]).astype(BF)
        part = jnp.sum(gated * gated, axis=1, keepdims=True)
        total = part if total is None else total + part
    if not first:
        total = total + prev[:, :1]
    if final:
        high = total.astype(BF)
        low = (total - high.astype(F32)).astype(BF)
        lane = lax.broadcasted_iota(jnp.int32, (total.shape[0], LANES), 1)
        out_ref[:, n_chunks * w :] = jnp.where(lane == 0, high.astype(F32), low.astype(F32)).astype(BF)
    else:
        ss_ref[...] = jnp.broadcast_to(total, ss_ref.shape)


def project_kernel(n_a, n_half, n_w, channels, sc, *refs):
    a_refs = refs[: n_a * n_half]
    own_ref = refs[n_a * n_half]
    w_refs = refs[n_a * n_half + 1 : n_a * n_half + 1 + n_w]
    out_ref = refs[n_a * n_half + 1 + n_w]
    sorted_ref, acc_ref, buf_ref, sem = refs[n_a * n_half + 2 + n_w :]
    rows = buf_ref.shape[1]
    for i in range(n_w):
        copy = pltpu.make_async_copy(w_refs[i], buf_ref.at[i], sem.at[i])

        @pl.when(sc[n_a + 3 * i] > 0)
        def _():
            copy.start()

    total = None
    for s in range(n_a):
        for h in range(n_half):
            a = a_refs[s * n_half + h]
            sorted_ref[sc[s] * n_half + h] = a[:, :rows]
        last = a_refs[s * n_half + n_half - 1]
        part = last[:, rows : rows + 1].astype(F32) + last[:, rows + 1 : rows + 2].astype(F32)
        total = part if total is None else total + part
    scale = lax.rsqrt(total / channels + 1e-5)
    own = sc[n_a + 3 * n_w]
    acc = None
    for h in range(n_half):
        part = dot(sorted_ref[own * n_half + h], own_ref[h * rows : (h + 1) * rows, :])
        acc = part if acc is None else acc + part
    acc_ref[...] = acc
    for i in range(n_w):
        copy = pltpu.make_async_copy(w_refs[i], buf_ref.at[i], sem.at[i])

        @pl.when(sc[n_a + 3 * i] > 0)
        def _():
            copy.wait()
            acc_ref[...] += dot(
                sorted_ref[sc[n_a + 3 * i + 1] * n_half + sc[n_a + 3 * i + 2]], buf_ref[i]
            )

    out_ref[...] = (acc_ref[...] * scale).astype(BF)


def shape(dims, dtype):
    return jax.ShapeDtypeStruct(dims, dtype)


def local(
    x_in, b_in, c_in, z_in, dt_raw, decay_rate, d_skip, conv_x, conv_b, conv_c, norm_gain, w_out
):
    tok = x_in.shape[0]
    all_heads = dt_raw.shape[1]
    head_size = x_in.shape[1] // all_heads
    n_state, n_head, n_ctx, n_group = [lax.axis_size(a) for a in ("state", "head", "ctx", "groups")]
    si, hi, ki, gi = [lax.axis_index(a) for a in ("state", "head", "ctx", "groups")]
    heads = all_heads // n_state
    width = heads * head_size
    nb = b_in.shape[1]
    n_all = nb * n_state
    channels = width * n_state * n_head
    phases = n_group
    per_phase = max(1, heads // (4 * phases))
    n_chunks = phases * per_phase
    cw = width // n_chunks
    send = lax.ppermute

    rows = w_out.shape[0] // n_group
    mine = lax.dynamic_slice_in_dim(w_out, gi * rows, rows, 0)

    rim = tok - HALO
    halo = jnp.concatenate(
        [lax.dynamic_slice(x_in, (rim, si * width), (HALO, width)), b_in[rim:], c_in[rim:]], axis=1
    )
    halo = send(halo, "ctx", line(n_ctx, 1))

    pieces = []
    right = left = mine
    for s in range(1, n_ctx):
        right = send(right, "ctx", line(n_ctx, 1))
        left = send(left, "ctx", line(n_ctx, -1))
        for held, ok, block in (
            (right, lambda k: k >= s, ki - s),
            (left, lambda k: k + s < n_ctx, ki + s),
        ):
            valid = (block >= 0) & (block < n_ctx)
            pieces.append((held, valid, block, gi))
            for d in range(1, n_group):
                route = [
                    (g * n_ctx + k, (g + d) % n_group * n_ctx + k)
                    for g in range(n_group)
                    for k in range(n_ctx)
                    if ok(k)
                ]
                pieces.append(
                    (send(held, ("groups", "ctx"), route), valid, block, (gi - d) % n_group)
                )

    dt = lax.dynamic_slice_in_dim(dt_raw, si * heads, heads, 1)
    decay = lax.dynamic_slice_in_dim(decay_rate.reshape(1, -1), si * heads, heads, 1)
    skip = lax.dynamic_slice_in_dim(d_skip.reshape(1, -1), si * heads, heads, 1)
    step, cum, cumt = pl.pallas_call(
        steps_kernel,
        out_shape=[shape((tok, heads), F32), shape((tok, heads), F32), shape((heads, tok), F32)],
        in_specs=[VM] * 2,
        out_specs=[VM] * 3,
        compiler_params=PARAMS,
        name="steps",
    )(dt, decay)

    def whole(a):
        return pl.BlockSpec(a.shape, lambda i, sc: (0,) * len(a.shape))

    part_rows = tok // n_head
    x_conv, bc, bc_part = pl.pallas_call(
        conv_kernel,
        grid_spec=pltpu.PrefetchScalarGridSpec(
            num_scalar_prefetch=1,
            grid=(1,),
            in_specs=[
                pl.BlockSpec((tok, width), lambda i, sc: (0, sc[0])),
                whole(b_in),
                whole(c_in),
                whole(halo),
                pl.BlockSpec((conv_x.shape[0], width), lambda i, sc: (0, sc[0])),
                whole(conv_b),
                whole(conv_c),
            ],
            out_specs=[
                pl.BlockSpec((tok, width), lambda i, sc: (0, 0)),
                pl.BlockSpec((tok, 2 * nb), lambda i, sc: (0, 0)),
                pl.BlockSpec((part_rows, 2 * nb), lambda i, sc: (0, 0)),
            ],
        ),
        out_shape=[
            shape((tok, width), BF),
            shape((tok, 2 * nb), BF),
            shape((part_rows, 2 * nb), BF),
        ],
        compiler_params=PARAMS,
        name="conv",
    )(jnp.stack([si, hi]).astype(jnp.int32), x_in, b_in, c_in, halo, conv_x, conv_b, conv_c)

    bcs = [bc]
    for j in range(1, n_state):
        got = send(bc_part, "state", ring(n_state, j))
        block = jnp.zeros((tok, 2 * nb), BF)
        block = lax.dynamic_update_slice_in_dim(block, got, hi * part_rows, 0)
        for d in range(1, n_head):
            other = send(got, "head", ring(n_head, d))
            block = lax.dynamic_update_slice_in_dim(
                block, other, (hi - d) % n_head * part_rows, 0
            )
        bcs.append(block)
    c_all = jnp.concatenate([b[:, nb:] for b in bcs], axis=1)
    c_next = send(c_all, "ctx", [(n_ctx - 1, n_ctx - 2)])

    outs = pl.pallas_call(
        functools.partial(states_kernel, n_state, n_chunks, head_size),
        out_shape=[shape((1, width), F32)]
        + [shape((n_all, cw), F32)] * n_chunks
        + [shape((n_all, cw), BF)] * n_chunks,
        in_specs=[VM] * (3 + n_state),
        out_specs=[VM] * (1 + 2 * n_chunks),
        compiler_params=PARAMS,
        name="states",
    )(x_conv, step, cum, *bcs)
    dec, full, first = outs[0], outs[1 : 1 + n_chunks], outs[1 + n_chunks :]
    decs = [dec[:, c * cw : (c + 1) * cw] for c in range(n_chunks)]

    enters = [[] for _ in range(n_chunks)]
    for hop in range(n_ctx - 2):
        for c in range(n_chunks):
            if hop == 0:
                message = first[c]
            else:
                message = (decs[c] * enters[c][-1].astype(F32) + full[c]).astype(BF)
            enters[c].append(send(message, "ctx", [(hop, hop + 1)]))
    lasts = []
    for c in range(n_chunks):
        args = [c_next, full[c], decs[c]] + enters[c][-1:]
        y = pl.pallas_call(
            functools.partial(last_hop_kernel, len(enters[c]) > 0, n_state),
            out_shape=shape((tok, cw), BF),
            in_specs=[VM] * len(args),
            out_specs=VM,
            compiler_params=PARAMS,
            name="last_hop",
        )(*args)
        lasts.append(send(y, "ctx", [(n_ctx - 2, n_ctx - 1)]))

    base = pl.pallas_call(
        functools.partial(intra_kernel, n_state, head_size),
        out_shape=shape((tok, width), F32),
        in_specs=[VM] * (5 + n_state),
        out_specs=VM,
        scratch_shapes=[pltpu.VMEM((tok, tok), F32), pltpu.VMEM((tok, width), BF)],
        compiler_params=PARAMS,
        name="intra",
    )(x_conv, step, cum, cumt, skip, *bcs)

    gain = norm_gain.reshape(1, -1)
    sources = [[] for _ in range(n_state * n_head)]
    prev = None
    pw = width // phases
    for ph in range(phases):
        chunk = range(ph * per_phase, (ph + 1) * per_phase)
        final = ph == phases - 1
        args = list(bcs) + [
            cum[:, ph * (heads // phases) : (ph + 1) * (heads // phases)],
            base[:, ph * pw : (ph + 1) * pw],
            z_in[:, ph * pw : (ph + 1) * pw],
            gain[:, ph * pw : (ph + 1) * pw],
        ]
        for c in chunk:
            args += enters[c]
        args += [lasts[c] for c in chunk]
        if ph:
            args.append(prev)
        out = pl.pallas_call(
            functools.partial(
                gate_kernel, n_state, n_ctx - 2, per_phase, head_size, ph == 0, final
            ),
            out_shape=shape((tok, pw + LANES), BF)
            if final
            else [shape((tok, pw), BF), shape((tok, LANES), F32)],
            in_specs=[VM] * len(args),
            out_specs=VM if final else [VM, VM],
            compiler_params=PARAMS,
            name="gate",
        )(*args)
        if not final:
            out, prev = out
        got = [out] + [send(out, "state", ring(n_state, j)) for j in range(1, n_state)]
        for d in range(n_head):
            for j in range(n_state):
                sources[d * n_state + j].append(
                    got[j] if d == 0 else send(got[j], "head", ring(n_head, d))
                )

    table = [
        (hi - d) % n_head * n_state + (si - j) % n_state
        for d in range(n_head)
        for j in range(n_state)
    ]
    for _, valid, block, half in pieces:
        table += [valid, jnp.clip(block, 0, n_ctx - 1), half]
    table.append(ki)
    table = jnp.stack([jnp.asarray(t, jnp.int32) for t in table])
    flat = [a for source in sources for a in source]
    n_a, n_w, out_width = len(sources), len(pieces), w_out.shape[1]
    return pl.pallas_call(
        functools.partial(project_kernel, n_a, phases, n_w, channels),
        out_shape=shape((tok, out_width), BF),
        in_specs=[SM] + [VM] * (len(flat) + 1) + [ANY] * n_w,
        out_specs=VM,
        scratch_shapes=[
            pltpu.VMEM((n_a * phases, tok, rows), BF),
            pltpu.VMEM((tok, out_width), F32),
            pltpu.VMEM((n_w, rows, out_width), BF),
            pltpu.SemaphoreType.DMA((n_w,)),
        ],
        compiler_params=PARAMS,
        name="project",
    )(table, *flat, w_out, *[p[0] for p in pieces])


def solution(mesh):
    return jax.shard_map(
        local,
        mesh=mesh,
        in_specs=(
            P(("groups", "ctx"), "head"),
            P(("groups", "ctx"), "state"),
            P(("groups", "ctx"), "state"),
            P(("groups", "ctx"), ("head", "state")),
            P(("groups", "ctx"), "head"),
            P("head"),
            P("head"),
            P(None, "head"),
            P(None, "state"),
            P(None, "state"),
            P(("head", "state")),
            P("ctx", ("state", "head")),
        ),
        out_specs=P(("groups", "ctx"), ("state", "head")),
        check_vma=False,
    )
```
